32 devices in a mesh: row: 4 (over z), col: 8 (over y, x, core).
Axes of the slice: x: 2, y: 2, z: 4, core: 2. Of those that a mesh axis runs over, the one named last changes fastest.
Arguments:
- right_side: float32 [64, 16384], P(None, ('row', 'col')), may hold values from -80 to 80
- diag_vals: float32 [16384], P(('row', 'col')), may hold values from 1.05 to 1.6
- tiles: bfloat16 [64, 16, 256, 256], P(('row', 'col')), may hold values from -1 to 1, as said below
- col_ids: int32 [64, 16], P(('row', 'col')), may hold values from 0 to 63, as said below
Outputs:
- solution: float32 [64, 16384], P(None, ('row', 'col'))
- residual: float32 [64, 16384], P(None, ('row', 'col'))
The draws below stay inside these ranges and needn't reach their ends.
Inputs may be any that keep to these rules, and one draw needn't show every extreme that they name: col_ids[i, m] = (i + o_m) mod 64 and col_ids[i, 8 + m] = (i - o_m) mod 64 for 8 distinct odd offsets o_m shared by all block-rows, each below 32. The pattern is symmetric. tiles[i, m] is the block in block-row i and block-column col_ids[i, m]; tiles[i, 8 + m] is the transpose of tiles[(i - o_m) mod 64, m], so the matrix is symmetric.
All inputs are finite; a program needn't handle non-finite values.
Results may differ from the reference program's by a relative error of at most 0.00062.
Values may be sent and summed in bfloat16 or wider, within the bound.
No kernel may reach another device: no remote copies, remote signals or barrier semaphores. Data moves between devices by JAX's collectives and lax.ppermute only.
A program may use at most 64 MiB of HBM per device.

```python
import jax
import jax.numpy as jnp
from jax import lax

BS = 256
S = 64
H = 8
ITERS = 4
K = 16
NB = 64
ORDER = 16384


def pick_offsets(key):
    order = jax.random.permutation(jax.random.fold_in(key, 7), NB // 8 - 1)
    rest = 4 * order[:H - 1].astype(jnp.int32) + 3
    far = jnp.full((1,), NB // 2 - 1, dtype=jnp.int32)
    return jnp.concatenate([far, rest]).astype(jnp.int32)


def draw_col_ids(key, part):
    offsets = pick_offsets(key)
    rows = jnp.arange(NB, dtype=jnp.int32)[:, None]
    upper = (rows + offsets[None, :]) % NB
    lower = (rows - offsets[None, :]) % NB
    return jnp.concatenate([upper, lower], axis=1).astype(jnp.int32)


def draw_tiles(key, part):
    offsets = pick_offsets(key)
    raw = jax.random.uniform(jax.random.fold_in(key, 11), (NB, H, BS, BS), dtype=jnp.float32)
    first = (jnp.arange(H, dtype=jnp.int32) == 0).astype(jnp.float32)[None, :, None, None]
    raw = first * (0.5 + 0.5 * raw) + (1.0 - first) * raw
    signs = jax.random.randint(jax.random.fold_in(key, 13), (NB, H, 1, 1), 0, 2).astype(jnp.float32) * 2.0 - 1.0
    base = raw * signs
    rows = jnp.arange(NB, dtype=jnp.int32)[:, None]
    source = (rows - offsets[None, :]) % NB
    which = jnp.arange(H, dtype=jnp.int32)[None, :]
    lower = jnp.swapaxes(base[source, which], 2, 3)
    return jnp.concatenate([base, lower], axis=1).astype(jnp.bfloat16)


def draw_right_side(key, part):
    spot = jnp.arange(ORDER, dtype=jnp.float32) / ORDER
    column = jnp.arange(S, dtype=jnp.float32) / S
    scale = (10.0 ** (spot - 0.5))[None, :] * (10.0 ** (column - 0.5))[:, None]
    level_key = jax.random.fold_in(key, 17)
    base = jnp.clip(jax.random.normal(key, (S, ORDER), dtype=jnp.float32), -3.0, 3.0)
    level = jnp.clip(jax.random.normal(level_key, (S, NB, 1), dtype=jnp.float32), -3.0, 3.0)
    level = jnp.broadcast_to(level, (S, NB, BS)).reshape(S, ORDER)
    return ((base + 1.5 * level) * scale).astype(jnp.float32)


def block_scale(own_key, extent, split, low, largest):
    def one(dim, shards_of):
        heights = jax.random.uniform(jax.random.fold_in(jax.random.fold_in(own_key, 6), dim), (shards_of,), jnp.float32, low / len(split), largest / len(split))
        return jnp.repeat(jnp.exp(heights), extent[dim] // shards_of).reshape((-1,) + (1,) * (len(extent) - dim - 1))

    loudness = one(*split[0])
    for cut in split[1:]:
        loudness = loudness * one(*cut)
    return loudness


def setup_inputs(seed: int = 0) -> dict:
    seeds = jax.random.split(jax.random.key(seed), 5)
    right_side = draw_right_side(jax.random.fold_in(seeds[4], 71), 0)
    diag_vals = jnp.clip(1.05 + 0.5500001 * jax.random.uniform(seeds[1], (ORDER,), jnp.float32) ** block_scale(seeds[1], (ORDER,), ((0, 32),), -0.2, 0.2), 1.05, 1.6)
    tiles = draw_tiles(jax.random.fold_in(seeds[4], 71), 0)
    col_ids = draw_col_ids(jax.random.fold_in(seeds[4], 71), 0)
    return dict(right_side=right_side, diag_vals=diag_vals, tiles=tiles, col_ids=col_ids)


def chol_solve(mat, rhs):
    lower = jnp.linalg.cholesky(mat)
    half = lax.linalg.triangular_solve(lower, rhs, left_side=True, lower=True)
    return lax.linalg.triangular_solve(lower, half, left_side=True, lower=True, transpose_a=True)

def apply_matrix(vec, diag_vals, tiles, col_ids):
    rounded = vec.astype(jnp.bfloat16).reshape(S, NB, BS)

    def one_row(args):
        block_tiles, ids = args
        picked = rounded[:, ids, :].astype(jnp.float32)
        return jnp.einsum('skb,kab->sa', picked, block_tiles.astype(jnp.float32))
    off = lax.map(one_row, (tiles, col_ids))
    off = jnp.transpose(off, (1, 0, 2)).reshape(S, ORDER)
    return diag_vals[None, :] * vec + 1.0 / (K * BS) * off

def gram_of(left, right):
    return jnp.dot(left.astype(jnp.float32), right.T.astype(jnp.float32), precision=lax.Precision.HIGHEST, preferred_element_type=jnp.float32)

def small_dot(left, right):
    return jnp.dot(left.astype(jnp.float32), right.astype(jnp.float32), precision=lax.Precision.HIGHEST, preferred_element_type=jnp.float32)

def reference(right_side, diag_vals, tiles, col_ids):
    solution = jnp.zeros_like(right_side)
    residual = right_side
    direction = right_side
    gram = gram_of(residual, residual)
    for step in range(ITERS):
        image = apply_matrix(direction, diag_vals, tiles, col_ids)
        curv = gram_of(direction, image)
        alpha = chol_solve(curv, gram)
        solution = solution + small_dot(alpha.T, direction)
        residual = residual - small_dot(alpha.T, image)
        if step + 1 < ITERS:
            gram_new = gram_of(residual, residual)
            beta = chol_solve(gram, gram_new)
            direction = residual + small_dot(beta.T, direction)
            gram = gram_new
    return (solution, residual)
```

```python
import functools

import jax
import jax.numpy as jnp
from jax import lax
from jax.experimental import pallas as pl
from jax.experimental.pallas import tpu as pltpu
from jax.sharding import PartitionSpec as P

ITERS = 4
AXES = ("row", "col")
HIGH = lax.Precision.HIGHEST


def nn(left, right):
    return lax.dot_general(
        left, right, (((1,), (0,)), ((), ())), precision=HIGH, preferred_element_type=jnp.float32
    )


def nt(left, right):
    return lax.dot_general(
        left, right, (((1,), (1,)), ((), ())), precision=HIGH, preferred_element_type=jnp.float32
    )


def xor_permute(val, mask, count):
    return lax.ppermute(val, AXES, [(i, i ^ mask) for i in range(count)])


def total_of(val, masks, count):
    for mask in masks:
        val = val + xor_permute(val, mask, count)
    return val


def gather_of(val, masks, count):
    for mask in masks:
        val = jnp.concatenate([val, xor_permute(val, mask, count)], axis=0)
    return val


def slot_of(diff, masks):
    slot = jnp.zeros_like(diff)
    for place, mask in enumerate(masks):
        slot = slot + jnp.where((diff & mask) != 0, 1 << place, 0)
    return slot


def matrix_kernel(rows, nbr, blk, chunk, slots, whole, tiles, vec, res, diag, image, grams, held, sems):
    coef = 1.0 / (nbr * blk)
    parts = rows * nbr // chunk
    copies = []
    for part in range(parts):
        row, first = divmod(part * chunk, nbr)
        copies.append(
            pltpu.make_async_copy(
                tiles.at[row, pl.ds(first, chunk)], held.at[pl.ds(part * chunk, chunk)], sems.at[part]
            )
        )
        copies[-1].start()
    for row in range(rows):
        acc = jnp.zeros((vec.shape[0], blk), jnp.float32)
        for k in range(nbr):
            spot = row * nbr + k
            if spot % chunk == 0:
                copies[spot // chunk].wait()
            acc = acc + lax.dot_general(
                whole[slots[spot]],
                held[spot],
                (((1,), (1,)), ((), ())),
                preferred_element_type=jnp.float32,
            )
        cols = pl.ds(row * blk, blk)
        image[:, cols] = diag[:, cols] * vec[:, cols] + coef * acc
    img = image[...]
    n = vec.shape[0]
    both = nt(jnp.concatenate([res[...], img], axis=0), jnp.concatenate([res[...], img], axis=0))
    grams[:, 0:n] = both[0:n, 0:n]
    grams[:, n : 2 * n] = nt(vec[...], img)
    grams[:, 2 * n : 3 * n] = both[0:n, n : 2 * n]
    grams[:, 3 * n : 4 * n] = both[n : 2 * n, n : 2 * n]


def apply_matrix(slots, whole, tiles, vec, res, diag):
    rows, nbr, blk, _ = tiles.shape
    n = vec.shape[0]
    chunk = 4
    space = pltpu.VMEM
    return pl.pallas_call(
        functools.partial(matrix_kernel, rows, nbr, blk, chunk),
        out_shape=(
            jax.ShapeDtypeStruct(vec.shape, jnp.float32),
            jax.ShapeDtypeStruct((n, 4 * n), jnp.float32),
        ),
        in_specs=[
            pl.BlockSpec(memory_space=pltpu.SMEM),
            pl.BlockSpec(memory_space=space),
            pl.BlockSpec(memory_space=pl.ANY),
            pl.BlockSpec(memory_space=space),
            pl.BlockSpec(memory_space=space),
            pl.BlockSpec(memory_space=space),
        ],
        out_specs=(pl.BlockSpec(memory_space=space), pl.BlockSpec(memory_space=space)),
        scratch_shapes=[
            pltpu.VMEM((rows * nbr, blk, blk), tiles.dtype),
            pltpu.SemaphoreType.DMA((rows * nbr // chunk,)),
        ],
        compiler_params=pltpu.CompilerParams(vmem_limit_bytes=40 * 1024 * 1024),
        name="matrix",
    )(slots, whole, tiles, vec, res, diag)


def invert_pair(mats, n):
    rows = lax.broadcasted_iota(jnp.int32, (n, 2 * n), 0)
    lanes = lax.broadcasted_iota(jnp.int32, (n, 2 * n), 1)
    left = lanes < n
    place = jnp.where(left, lanes, lanes - n)
    for j in range(n):
        col = jnp.where(
            left,
            jnp.broadcast_to(mats[:, j : j + 1], (n, 2 * n)),
            jnp.broadcast_to(mats[:, n + j : n + j + 1], (n, 2 * n)),
        )
        pivot = col[j : j + 1, :]
        inv = 1.0 / pivot
        line = mats[j : j + 1, :]
        scaled = jnp.where(place[0:1, :] == j, inv, line * inv)
        kept = jnp.where(place == j, 0.0, mats)
        mats = jnp.where(rows == j, jnp.broadcast_to(scaled, (n, 2 * n)), kept - col * scaled)
    return mats


def solve_kernel(last, grams, other, vec, res, sol, image, *outs):
    n = vec.shape[0]
    full = grams[...] + other[...]
    gram, curv = full[:, 0:n], full[:, n : 2 * n]
    inverses = invert_pair(jnp.concatenate([curv, gram], axis=1), n)
    alpha_t = nn(gram, inverses[:, 0:n])
    old = vec[...]
    new = res[...] - nn(alpha_t, image[...])
    outs[0][...] = sol[...] + nn(alpha_t, old)
    outs[1][...] = new
    if not last:
        cross, square = full[:, 2 * n : 3 * n], full[:, 3 * n : 4 * n]
        mixed = nt(cross, alpha_t)
        gram_new = gram - mixed + nn(alpha_t, nt(square, alpha_t) - cross.T)
        beta_t = nn(gram_new, inverses[:, n : 2 * n])
        step = new + nn(beta_t, old)
        outs[2][...] = step
        blk = outs[3].shape[2]
        for row in range(outs[3].shape[0]):
            outs[3][row] = step[:, row * blk : (row + 1) * blk].astype(jnp.bfloat16)


def solve_step(last, rows, grams, other, vec, res, sol, image):
    shape = jax.ShapeDtypeStruct(vec.shape, jnp.float32)
    n, width = vec.shape
    space = pl.BlockSpec(memory_space=pltpu.VMEM)
    outs = [shape, shape]
    if not last:
        outs += [shape, jax.ShapeDtypeStruct((rows, n, width // rows), jnp.bfloat16)]
    return pl.pallas_call(
        functools.partial(solve_kernel, last),
        out_shape=tuple(outs),
        in_specs=[space] * 6,
        out_specs=tuple([space] * len(outs)),
        name="small_last" if last else "small",
    )(grams, other, vec, res, sol, image)


def body(gather_masks, sum_masks, count, cols, right_side, diag_vals, tiles, col_ids):
    rows, nbr, blk, _ = tiles.shape
    n = right_side.shape[0]
    me = lax.axis_index("row") * cols + lax.axis_index("col")
    ids = col_ids.reshape(-1)
    slots = slot_of(me ^ (ids // rows), gather_masks) * rows + ids % rows
    diag = diag_vals[None, :]
    sol = jnp.zeros_like(right_side)
    res = right_side
    vec = right_side
    rounded = right_side.astype(jnp.bfloat16).reshape(n, rows, blk).transpose(1, 0, 2)
    for step in range(ITERS):
        last = step + 1 == ITERS
        whole = gather_of(rounded, gather_masks, count)
        image, grams = apply_matrix(slots, whole, tiles, vec, res, diag)
        if last:
            grams = grams[:, : 2 * n]
        part = total_of(grams, sum_masks[:-1], count)
        outs = solve_step(last, rows, part, xor_permute(part, sum_masks[-1], count), vec, res, sol, image)
        if last:
            sol, res = outs
        else:
            sol, res, vec, rounded = outs
    return (sol, res)


def solution(mesh):
    placed = (
        P(None, ("row", "col")),
        P(("row", "col")),
        P(("row", "col"), None, None, None),
        P(("row", "col"), None),
    )
    count = mesh.shape["row"] * mesh.shape["col"]
    cols = mesh.shape["col"]
    bits = [1 << i for i in range(count.bit_length() - 1)]
    major = [b for b in bits if b >= cols]
    minor = [b for b in bits if 1 < b < cols]
    return jax.shard_map(
        functools.partial(body, major + minor + [1], bits, count, cols),
        mesh=mesh,
        in_specs=placed,
        out_specs=(P(None, ("row", "col")), P(None, ("row", "col"))),
        check_vma=False,
    )
```

```python
import functools

import jax
import jax.numpy as jnp
from jax import lax
from jax.experimental import pallas as pl
from jax.experimental.pallas import tpu as pltpu
from jax.sharding import PartitionSpec as P

ITERS = 4
AXES = ("row", "col")
HIGH = lax.Precision.HIGHEST


def nn(left, right):
    return lax.dot_general(
        left, right, (((1,), (0,)), ((), ())), precision=HIGH, preferred_element_type=jnp.float32
    )


def nt(left, right):
    return lax.dot_general(
        left, right, (((1,), (1,)), ((), ())), precision=HIGH, preferred_element_type=jnp.float32
    )


def xor_permute(val, mask, count):
    return lax.ppermute(val, AXES, [(i, i ^ mask) for i in range(count)])


def spread(val, masks, count):
    partners = [0]
    for mask in masks:
        partners = partners + [p ^ mask for p in partners]
    return [val] + [xor_permute(val, p, count) for p in partners[1:]]


def gather_of(val, groups, core, count):
    for masks in groups[:-1]:
        val = jnp.concatenate(spread(val, masks, count), axis=0)
    pieces = spread(val, groups[-1], count)
    return pieces + [xor_permute(piece, core, count) for piece in pieces]


def slot_of(diff, masks):
    slot = jnp.zeros_like(diff)
    for place, mask in enumerate(masks):
        slot = slot + jnp.where((diff & mask) != 0, 1 << place, 0)
    return slot


def matrix_kernel(rows, nbr, blk, chunk, count, slots, tiles, vec, res, diag, *refs):
    pieces, (image, keep, give, held, whole, sems, piece_sems) = refs[:count], refs[count:]
    coef = 1.0 / (nbr * blk)
    parts = rows * nbr // chunk
    each = whole.shape[0] // count
    arrivals = [
        pltpu.make_async_copy(piece, whole.at[pl.ds(i * each, each)], piece_sems.at[i])
        for i, piece in enumerate(pieces)
    ]
    copies = []
    for part in range(parts):
        row, first = divmod(part * chunk, nbr)
        copies.append(
            pltpu.make_async_copy(
                tiles.at[row, pl.ds(first, chunk)], held.at[pl.ds(part * chunk, chunk)], sems.at[part]
            )
        )
    for copy in arrivals + copies:
        copy.start()
    for copy in arrivals:
        copy.wait()
    n = vec.shape[0]
    for row in range(rows):
        acc = jnp.zeros((n, blk), jnp.float32)
        for k in range(nbr):
            spot = row * nbr + k
            if spot % chunk == 0:
                copies[spot // chunk].wait()
            acc = acc + lax.dot_general(
                whole[slots[spot]],
                held[spot],
                (((1,), (1,)), ((), ())),
                preferred_element_type=jnp.float32,
            )
        cols = pl.ds(row * blk, blk)
        image[:, cols] = diag[:, cols] * vec[:, cols] + coef * acc
    img = image[...]
    old = res[...]
    both = nt(jnp.concatenate([old, img], axis=0), jnp.concatenate([old, img], axis=0))
    curv = nt(vec[...], img)
    first = jnp.concatenate([both[0:n, 0:n], curv], axis=1)
    second = both[:, n : 2 * n]
    second = jnp.concatenate([second[0:n], second[n : 2 * n]], axis=1)
    core = slots[rows * nbr]
    keep[...] = jnp.where(core == 0, first, second)
    give[...] = jnp.where(core == 0, second, first)


def apply_matrix(slots, pieces, tiles, vec, res, diag):
    rows, nbr, blk, _ = tiles.shape
    n = vec.shape[0]
    chunk = 4
    vmem = pl.BlockSpec(memory_space=pltpu.VMEM)
    anywhere = pl.BlockSpec(memory_space=pl.ANY)
    half = jax.ShapeDtypeStruct((n, 2 * n), jnp.float32)
    blocks = sum(piece.shape[0] for piece in pieces)
    return pl.pallas_call(
        functools.partial(matrix_kernel, rows, nbr, blk, chunk, len(pieces)),
        out_shape=(jax.ShapeDtypeStruct(vec.shape, jnp.float32), half, half),
        in_specs=[pl.BlockSpec(memory_space=pltpu.SMEM), anywhere, vmem, vmem, vmem]
        + [anywhere] * len(pieces),
        out_specs=(vmem, vmem, vmem),
        scratch_shapes=[
            pltpu.VMEM((rows * nbr, blk, blk), tiles.dtype),
            pltpu.VMEM((blocks, n, blk), tiles.dtype),
            pltpu.SemaphoreType.DMA((rows * nbr // chunk,)),
            pltpu.SemaphoreType.DMA((len(pieces),)),
        ],
        compiler_params=pltpu.CompilerParams(vmem_limit_bytes=40 * 1024 * 1024),
        name="matrix",
    )(slots, tiles, vec, res, diag, *pieces)


def invert_pair(mats, n):
    rows = lax.broadcasted_iota(jnp.int32, (n, 2 * n), 0)
    lanes = lax.broadcasted_iota(jnp.int32, (n, 2 * n), 1)
    left = lanes < n
    place = jnp.where(left, lanes, lanes - n)
    for j in range(n):
        col = jnp.where(
            left,
            jnp.broadcast_to(mats[:, j : j + 1], (n, 2 * n)),
            jnp.broadcast_to(mats[:, n + j : n + j + 1], (n, 2 * n)),
        )
        pivot = col[j : j + 1, :]
        inv = 1.0 / pivot
        line = mats[j : j + 1, :]
        scaled = jnp.where(place[0:1, :] == j, inv, line * inv)
        kept = jnp.where(place == j, 0.0, mats)
        mats = jnp.where(rows == j, jnp.broadcast_to(scaled, (n, 2 * n)), kept - col * scaled)
    return mats


def solve_kernel(last, core, mine, other, vec, res, sol, image, *outs):
    n = vec.shape[0]
    at_zero = core[0] == 0
    first = jnp.where(at_zero, mine[...], other[...])
    gram, curv = first[:, 0:n], first[:, n : 2 * n]
    inverses = invert_pair(jnp.concatenate([curv, gram], axis=1), n)
    alpha_t = nn(gram, inverses[:, 0:n])
    old = vec[...]
    new = res[...] - nn(alpha_t, image[...])
    outs[0][...] = sol[...] + nn(alpha_t, old)
    outs[1][...] = new
    if not last:
        second = jnp.where(at_zero, other[...], mine[...])
        cross, square = second[:, 0:n], second[:, n : 2 * n]
        mixed = nt(cross, alpha_t)
        gram_new = gram - mixed + nn(alpha_t, nt(square, alpha_t) - cross.T)
        beta_t = nn(gram_new, inverses[:, n : 2 * n])
        step = new + nn(beta_t, old)
        outs[2][...] = step
        blk = outs[3].shape[2]
        for row in range(outs[3].shape[0]):
            outs[3][row] = step[:, row * blk : (row + 1) * blk].astype(jnp.bfloat16)


def solve_step(last, rows, core, mine, other, vec, res, sol, image):
    shape = jax.ShapeDtypeStruct(vec.shape, jnp.float32)
    n, width = vec.shape
    space = pl.BlockSpec(memory_space=pltpu.VMEM)
    outs = [shape, shape]
    if not last:
        outs += [shape, jax.ShapeDtypeStruct((rows, n, width // rows), jnp.bfloat16)]
    return pl.pallas_call(
        functools.partial(solve_kernel, last),
        out_shape=tuple(outs),
        in_specs=[pl.BlockSpec(memory_space=pltpu.SMEM)] + [space] * 6,
        out_specs=tuple([space] * len(outs)),
        name="small_last" if last else "small",
    )(core, mine, other, vec, res, sol, image)


def body(groups, bits, core_bit, count, cols, right_side, diag_vals, tiles, col_ids):
    rows, nbr, blk, _ = tiles.shape
    n = right_side.shape[0]
    me = lax.axis_index("row") * cols + lax.axis_index("col")
    core = ((me & core_bit) != 0).astype(jnp.int32)[None]
    ids = col_ids.reshape(-1)
    order = [mask for masks in groups for mask in masks] + [core_bit]
    slots = slot_of(me ^ (ids // rows), order) * rows + ids % rows
    slots = jnp.concatenate([slots, core])
    diag = diag_vals[None, :]
    sol = jnp.zeros_like(right_side)
    res = right_side
    vec = right_side
    rounded = right_side.astype(jnp.bfloat16).reshape(n, rows, blk).transpose(1, 0, 2)
    for step in range(ITERS):
        last = step + 1 == ITERS
        pieces = gather_of(rounded, groups, core_bit, count)
        image, keep, give = apply_matrix(slots, pieces, tiles, vec, res, diag)
        mine = keep + xor_permute(give, core_bit, count)
        for mask in bits:
            mine = mine + xor_permute(mine, mask, count)
        other = xor_permute(mine, core_bit, count)
        outs = solve_step(last, rows, core, mine, other, vec, res, sol, image)
        if last:
            sol, res = outs
        else:
            sol, res, vec, rounded = outs
    return (sol, res)


def solution(mesh):
    placed = (
        P(None, ("row", "col")),
        P(("row", "col")),
        P(("row", "col"), None, None, None),
        P(("row", "col"), None),
    )
    count = mesh.shape["row"] * mesh.shape["col"]
    cols = mesh.shape["col"]
    bits = [1 << i for i in range(1, count.bit_length() - 1)]
    major = [b for b in bits if b >= cols]
    minor = [b for b in bits if b < cols]
    groups = [part[i : i + 2] for part in (major, minor) for i in range(0, len(part), 2)]
    return jax.shard_map(
        functools.partial(body, groups, bits, 1, count, cols),
        mesh=mesh,
        in_specs=placed,
        out_specs=(P(None, ("row", "col")), P(None, ("row", "col"))),
        check_vma=False,
    )
```

```python
import functools

import jax
import jax.numpy as jnp
from jax import lax
from jax.experimental import pallas as pl
from jax.experimental.pallas import tpu as pltpu
from jax.sharding import PartitionSpec as P

ITERS = 4
AXES = ("row", "col")
HIGH = lax.Precision.HIGHEST


def nn(left, right):
    return lax.dot_general(
        left, right, (((1,), (0,)), ((), ())), precision=HIGH, preferred_element_type=jnp.float32
    )


def nt(left, right):
    return lax.dot_general(
        left, right, (((1,), (1,)), ((), ())), precision=HIGH, preferred_element_type=jnp.float32
    )


def xor_permute(val, mask, count):
    return lax.ppermute(val, AXES, [(i, i ^ mask) for i in range(count)])


def spread(val, masks, count):
    partners = [0]
    for mask in masks:
        partners = partners + [p ^ mask for p in partners]
    return [val] + [xor_permute(val, p, count) for p in partners[1:]]


def crossed_permute(val, even, odd, core, count):
    return lax.ppermute(val, AXES, [(i, i ^ (odd if i & core else even)) for i in range(count)])


def gather_of(val, groups, crossed, core, count):
    for masks in groups:
        val = jnp.concatenate(spread(val, masks, count), axis=0)
    one, two = crossed
    near = crossed_permute(val, one, two, core, count)
    far = crossed_permute(val, two, one, core, count)
    both = crossed_permute(near, two, one, core, count)
    pieces = [val, near, far, both]
    return pieces + [xor_permute(piece, core, count) for piece in pieces]


def slot_of(me, other, groups, crossed, core):
    diff = me ^ other
    slot = jnp.zeros_like(diff)
    place = 1
    for masks in groups:
        for mask in masks:
            slot = slot + jnp.where((diff & mask) != 0, place, 0)
            place *= 2
    one, two = crossed
    at_one = (other & core) != 0
    first = jnp.where(at_one, diff & two, diff & one) != 0
    second = jnp.where(at_one, diff & one, diff & two) != 0
    slot = slot + jnp.where(first, place, 0) + jnp.where(second, 2 * place, 0)
    return slot + jnp.where((diff & core) != 0, 4 * place, 0)


def matrix_kernel(rows, nbr, blk, count, slots, tiles, vec, res, diag, *refs):
    pieces, (image, keep, give, whole, piece_sems) = refs[:count], refs[count:]
    coef = 1.0 / (nbr * blk)
    each = whole.shape[0] // count
    arrivals = [
        pltpu.make_async_copy(piece, whole.at[pl.ds(i * each, each)], piece_sems.at[i])
        for i, piece in enumerate(pieces)
    ]
    for copy in arrivals:
        copy.start()
    for copy in arrivals:
        copy.wait()
    n = vec.shape[0]
    for row in range(rows):
        acc = jnp.zeros((n, blk), jnp.float32)
        for k in range(nbr):
            spot = row * nbr + k
            acc = acc + lax.dot_general(
                whole[slots[spot]],
                tiles[row, k],
                (((1,), (1,)), ((), ())),
                preferred_element_type=jnp.float32,
            )
        cols = pl.ds(row * blk, blk)
        image[:, cols] = diag[:, cols] * vec[:, cols] + coef * acc
    img = image[...]
    old = res[...]
    both = nt(jnp.concatenate([old, img], axis=0), jnp.concatenate([old, img], axis=0))
    curv = nt(vec[...], img)
    first = jnp.concatenate([both[0:n, 0:n], curv], axis=1)
    second = both[:, n : 2 * n]
    second = jnp.concatenate([second[0:n], second[n : 2 * n]], axis=1)
    core = slots[rows * nbr]
    keep[...] = jnp.where(core == 0, first, second)
    give[...] = jnp.where(core == 0, second, first)


def apply_matrix(slots, pieces, tiles, vec, res, diag):
    rows, nbr, blk, _ = tiles.shape
    n = vec.shape[0]
    vmem = pl.BlockSpec(memory_space=pltpu.VMEM)
    anywhere = pl.BlockSpec(memory_space=pl.ANY)
    half = jax.ShapeDtypeStruct((n, 2 * n), jnp.float32)
    blocks = sum(piece.shape[0] for piece in pieces)
    return pl.pallas_call(
        functools.partial(matrix_kernel, rows, nbr, blk, len(pieces)),
        out_shape=(jax.ShapeDtypeStruct(vec.shape, jnp.float32), half, half),
        in_specs=[pl.BlockSpec(memory_space=pltpu.SMEM), vmem, vmem, vmem, vmem]
        + [anywhere] * len(pieces),
        out_specs=(vmem, vmem, vmem),
        scratch_shapes=[
            pltpu.VMEM((blocks, n, blk), tiles.dtype),
            pltpu.SemaphoreType.DMA((len(pieces),)),
        ],
        compiler_params=pltpu.CompilerParams(vmem_limit_bytes=12 * 1024 * 1024),
        name="matrix",
    )(slots, tiles, vec, res, diag, *pieces)


def invert_pair(mats, n):
    rows = lax.broadcasted_iota(jnp.int32, (n, 2 * n), 0)
    lanes = lax.broadcasted_iota(jnp.int32, (n, 2 * n), 1)
    left = lanes < n
    place = jnp.where(left, lanes, lanes - n)
    for j in range(n):
        col = jnp.where(
            left,
            jnp.broadcast_to(mats[:, j : j + 1], (n, 2 * n)),
            jnp.broadcast_to(mats[:, n + j : n + j + 1], (n, 2 * n)),
        )
        pivot = col[j : j + 1, :]
        inv = 1.0 / pivot
        line = mats[j : j + 1, :]
        scaled = jnp.where(place[0:1, :] == j, inv, line * inv)
        kept = jnp.where(place == j, 0.0, mats)
        mats = jnp.where(rows == j, jnp.broadcast_to(scaled, (n, 2 * n)), kept - col * scaled)
    return mats


def solve_kernel(last, core, mine, other, vec, res, sol, image, *outs):
    n = vec.shape[0]
    at_zero = core[0] == 0
    first = jnp.where(at_zero, mine[...], other[...])
    gram, curv = first[:, 0:n], first[:, n : 2 * n]
    inverses = invert_pair(jnp.concatenate([curv, gram], axis=1), n)
    alpha_t = nn(gram, inverses[:, 0:n])
    old = vec[...]
    new = res[...] - nn(alpha_t, image[...])
    outs[0][...] = sol[...] + nn(alpha_t, old)
    outs[1][...] = new
    if not last:
        second = jnp.where(at_zero, other[...], mine[...])
        cross, square = second[:, 0:n], second[:, n : 2 * n]
        mixed = nt(cross, alpha_t)
        gram_new = gram - mixed + nn(alpha_t, nt(square, alpha_t) - cross.T)
        beta_t = nn(gram_new, inverses[:, n : 2 * n])
        step = new + nn(beta_t, old)
        outs[2][...] = step
        blk = outs[3].shape[2]
        for row in range(outs[3].shape[0]):
            outs[3][row] = step[:, row * blk : (row + 1) * blk].astype(jnp.bfloat16)


def solve_step(last, rows, core, mine, other, vec, res, sol, image):
    shape = jax.ShapeDtypeStruct(vec.shape, jnp.float32)
    n, width = vec.shape
    space = pl.BlockSpec(memory_space=pltpu.VMEM)
    outs = [shape, shape]
    if not last:
        outs += [shape, jax.ShapeDtypeStruct((rows, n, width // rows), jnp.bfloat16)]
    return pl.pallas_call(
        functools.partial(solve_kernel, last),
        out_shape=tuple(outs),
        in_specs=[pl.BlockSpec(memory_space=pltpu.SMEM)] + [space] * 6,
        out_specs=tuple([space] * len(outs)),
        compiler_params=pltpu.CompilerParams(vmem_limit_bytes=8 * 1024 * 1024),
        name="small_last" if last else "small",
    )(core, mine, other, vec, res, sol, image)


def body(groups, crossed, bits, core_bit, count, cols, right_side, diag_vals, tiles, col_ids):
    rows, nbr, blk, _ = tiles.shape
    n = right_side.shape[0]
    me = lax.axis_index("row") * cols + lax.axis_index("col")
    core = ((me & core_bit) != 0).astype(jnp.int32)[None]
    ids = col_ids.reshape(-1)
    slots = slot_of(me, ids // rows, groups, crossed, core_bit) * rows + ids % rows
    slots = jnp.concatenate([slots, core])
    diag = diag_vals[None, :]
    sol = jnp.zeros_like(right_side)
    res = right_side
    vec = right_side
    rounded = right_side.astype(jnp.bfloat16).reshape(n, rows, blk).transpose(1, 0, 2)
    for step in range(ITERS):
        last = step + 1 == ITERS
        pieces = gather_of(rounded, groups, crossed, core_bit, count)
        image, keep, give = apply_matrix(slots, pieces, tiles, vec, res, diag)
        mine = keep + xor_permute(give, core_bit, count)
        for mask in bits:
            mine = mine + xor_permute(mine, mask, count)
        other = xor_permute(mine, core_bit, count)
        outs = solve_step(last, rows, core, mine, other, vec, res, sol, image)
        if last:
            sol, res = outs
        else:
            sol, res, vec, rounded = outs
    return (sol, res)


def solution(mesh):
    placed = (
        P(None, ("row", "col")),
        P(("row", "col")),
        P(("row", "col"), None, None, None),
        P(("row", "col"), None),
    )
    count = mesh.shape["row"] * mesh.shape["col"]
    cols = mesh.shape["col"]
    bits = [1 << i for i in range(1, count.bit_length() - 1)]
    crossed, rest = bits[:2], bits[2:]
    major = [b for b in rest if b >= cols]
    minor = [b for b in rest if b < cols]
    groups = [part[i : i + 2] for part in (major, minor) for i in range(0, len(part), 2)]
    return jax.shard_map(
        functools.partial(body, groups, crossed, bits, 1, count, cols),
        mesh=mesh,
        in_specs=placed,
        out_specs=(P(None, ("row", "col")), P(None, ("row", "col"))),
        check_vma=False,
    )
```

```python
import functools

import jax
import jax.numpy as jnp
from jax import lax
from jax.experimental import pallas as pl
from jax.experimental.pallas import tpu as pltpu
from jax.sharding import PartitionSpec as P

ITERS = 4
AXES = ("row", "col")
HIGH = lax.Precision.HIGHEST


def nn(left, right):
    return lax.dot_general(
        left, right, (((1,), (0,)), ((), ())), precision=HIGH, preferred_element_type=jnp.float32
    )


def nt(left, right):
    return lax.dot_general(
        left, right, (((1,), (1,)), ((), ())), precision=HIGH, preferred_element_type=jnp.float32
    )


def xor_permute(val, mask, count):
    return lax.ppermute(val, AXES, [(i, i ^ mask) for i in range(count)])


def spread(val, masks, count):
    partners = [0]
    for mask in masks:
        partners = partners + [p ^ mask for p in partners]
    return [val] + [xor_permute(val, p, count) for p in partners[1:]]


def crossed_permute(val, even, odd, core, count):
    return lax.ppermute(val, AXES, [(i, i ^ (odd if i & core else even)) for i in range(count)])


def gather_of(val, groups, crossed, core, count):
    for masks in groups[:-1]:
        val = jnp.concatenate(spread(val, masks, count), axis=0)
    parts = spread(val, groups[-1], count)
    half = len(parts) // 2
    halves = [jnp.concatenate(parts[:half], axis=0), jnp.concatenate(parts[half:], axis=0)]
    one, two = crossed
    near = [crossed_permute(part, one, two, core, count) for part in halves]
    far = [crossed_permute(part, two, one, core, count) for part in halves]
    both = [crossed_permute(part, two, one, core, count) for part in near]
    pieces = halves + near + far + both
    return pieces + [xor_permute(piece, core, count) for piece in pieces]


def slot_of(me, other, groups, crossed, core):
    diff = me ^ other
    slot = jnp.zeros_like(diff)
    place = 1
    for masks in groups:
        for mask in masks:
            slot = slot + jnp.where((diff & mask) != 0, place, 0)
            place *= 2
    one, two = crossed
    at_one = (other & core) != 0
    first = jnp.where(at_one, diff & two, diff & one) != 0
    second = jnp.where(at_one, diff & one, diff & two) != 0
    slot = slot + jnp.where(first, place, 0) + jnp.where(second, 2 * place, 0)
    return slot + jnp.where((diff & core) != 0, 4 * place, 0)


def matrix_kernel(rows, nbr, blk, count, slots, tiles, vec, res, diag, *refs):
    pieces, (image, keep, give, whole, piece_sems) = refs[:count], refs[count:]
    coef = 1.0 / (nbr * blk)
    each = whole.shape[0] // count
    arrivals = [
        pltpu.make_async_copy(piece, whole.at[pl.ds(i * each, each)], piece_sems.at[i])
        for i, piece in enumerate(pieces)
    ]
    for copy in arrivals:
        copy.start()
    for copy in arrivals:
        copy.wait()
    n = vec.shape[0]
    for row in range(rows):
        acc = jnp.zeros((n, blk), jnp.float32)
        for k in range(nbr):
            spot = row * nbr + k
            acc = acc + lax.dot_general(
                whole[slots[spot]],
                tiles[row, k],
                (((1,), (1,)), ((), ())),
                preferred_element_type=jnp.float32,
            )
        cols = pl.ds(row * blk, blk)
        image[:, cols] = diag[:, cols] * vec[:, cols] + coef * acc
    img = image[...]
    old = res[...]
    both = nt(jnp.concatenate([old, img], axis=0), jnp.concatenate([old, img], axis=0))
    curv = nt(vec[...], img)
    first = jnp.concatenate([both[0:n, 0:n], curv], axis=1)
    second = both[:, n : 2 * n]
    second = jnp.concatenate([second[0:n], second[n : 2 * n]], axis=1)
    core = slots[rows * nbr]
    keep[...] = jnp.where(core == 0, first, second)
    give[...] = jnp.where(core == 0, second, first)


def round_kernel(source, target, same):
    blk = target.shape[2]
    for row in range(target.shape[0]):
        target[row] = source[:, row * blk : (row + 1) * blk].astype(jnp.bfloat16)
    same[...] = source[...]


def round_blocks(source, rows):
    n, width = source.shape
    vmem = pl.BlockSpec(memory_space=pltpu.VMEM)
    return pl.pallas_call(
        round_kernel,
        out_shape=(
            jax.ShapeDtypeStruct((rows, n, width // rows), jnp.bfloat16),
            jax.ShapeDtypeStruct(source.shape, source.dtype),
        ),
        in_specs=[vmem],
        out_specs=(vmem, vmem),
        compiler_params=pltpu.CompilerParams(vmem_limit_bytes=4 * 1024 * 1024),
        name="round",
    )(source)


def apply_matrix(slots, pieces, tiles, vec, res, diag):
    rows, nbr, blk, _ = tiles.shape
    n = vec.shape[0]
    vmem = pl.BlockSpec(memory_space=pltpu.VMEM)
    anywhere = pl.BlockSpec(memory_space=pl.ANY)
    half = jax.ShapeDtypeStruct((n, 2 * n), jnp.float32)
    blocks = sum(piece.shape[0] for piece in pieces)
    return pl.pallas_call(
        functools.partial(matrix_kernel, rows, nbr, blk, len(pieces)),
        out_shape=(jax.ShapeDtypeStruct(vec.shape, jnp.float32), half, half),
        in_specs=[pl.BlockSpec(memory_space=pltpu.SMEM), vmem, vmem, vmem, vmem]
        + [anywhere] * len(pieces),
        out_specs=(vmem, vmem, vmem),
        scratch_shapes=[
            pltpu.VMEM((blocks, n, blk), tiles.dtype),
            pltpu.SemaphoreType.DMA((len(pieces),)),
        ],
        compiler_params=pltpu.CompilerParams(vmem_limit_bytes=12 * 1024 * 1024),
        name="matrix",
    )(slots, tiles, vec, res, diag, *pieces)


def invert_pair(mats, n):
    size = 8
    width = 2 * n
    lanes = lax.broadcasted_iota(jnp.int32, (size, width), 1)
    rows = lax.broadcasted_iota(jnp.int32, (size, width), 0)
    left = lanes < n
    place = jnp.where(left, lanes, lanes - n)
    line_place = place[0:1, :]
    blocks = [mats[i : i + size, :] for i in range(0, n, size)]
    for at in range(n // size):
        base = at * size
        spread_cols = [
            [
                jnp.where(
                    left,
                    jnp.broadcast_to(block[:, base + i : base + i + 1], (size, width)),
                    jnp.broadcast_to(block[:, n + base + i : n + base + i + 1], (size, width)),
                )
                for i in range(size)
            ]
            for block in blocks
        ]
        own = spread_cols[at]
        inside = (line_place >= base) & (line_place < base + size)
        lines = [
            jnp.where(line_place == base + i, 1.0, jnp.where(inside, 0.0, blocks[at][i : i + 1, :]))
            for i in range(size)
        ]
        upper = [[own[k][i : i + 1, :] if k >= i else None for k in range(size)] for i in range(size)]
        for i in range(size):
            inv = 1.0 / upper[i][i]
            for m in range(i + 1, size):
                factor = upper[i][m] * inv
                for k in range(m, size):
                    upper[m][k] = upper[m][k] - factor * upper[i][k]
                lines[m] = lines[m] - factor * lines[i]
            upper[i][i] = inv
        for i in reversed(range(size)):
            for k in range(i + 1, size):
                lines[i] = lines[i] - upper[i][k] * lines[k]
            lines[i] = lines[i] * upper[i][i]
        within = (place >= base) & (place < base + size)
        solved = jnp.broadcast_to(lines[0], (size, width))
        for i in range(1, size):
            solved = jnp.where(rows == i, jnp.broadcast_to(lines[i], (size, width)), solved)
        for q, block in enumerate(blocks):
            if q == at:
                continue
            kept = jnp.where(within, 0.0, block)
            for i in range(size):
                kept = kept - spread_cols[q][i] * lines[i]
            blocks[q] = kept
        blocks[at] = solved
    return jnp.concatenate(blocks, axis=0)


def solve_kernel(last, core, mine, other, vec, res, sol, image, *outs):
    n = vec.shape[0]
    at_zero = core[0] == 0
    first = jnp.where(at_zero, mine[...], other[...])
    gram, curv = first[:, 0:n], first[:, n : 2 * n]
    inverses = invert_pair(jnp.concatenate([curv, gram], axis=1), n)
    alpha_t = nn(gram, inverses[:, 0:n])
    old = vec[...]
    new = res[...] - nn(alpha_t, image[...])
    outs[0][...] = sol[...] + nn(alpha_t, old)
    outs[1][...] = new
    if not last:
        second = jnp.where(at_zero, other[...], mine[...])
        cross, square = second[:, 0:n], second[:, n : 2 * n]
        mixed = nt(cross, alpha_t)
        gram_new = gram - mixed + nn(alpha_t, nt(square, alpha_t) - cross.T)
        beta_t = nn(gram_new, inverses[:, n : 2 * n])
        step = new + nn(beta_t, old)
        outs[2][...] = step
        blk = outs[3].shape[2]
        for row in range(outs[3].shape[0]):
            outs[3][row] = step[:, row * blk : (row + 1) * blk].astype(jnp.bfloat16)


def solve_step(last, rows, core, mine, other, vec, res, sol, image):
    shape = jax.ShapeDtypeStruct(vec.shape, jnp.float32)
    n, width = vec.shape
    space = pl.BlockSpec(memory_space=pltpu.VMEM)
    outs = [shape, shape]
    if not last:
        outs += [shape, jax.ShapeDtypeStruct((rows, n, width // rows), jnp.bfloat16)]
    return pl.pallas_call(
        functools.partial(solve_kernel, last),
        out_shape=tuple(outs),
        in_specs=[pl.BlockSpec(memory_space=pltpu.SMEM)] + [space] * 6,
        out_specs=tuple([space] * len(outs)),
        compiler_params=pltpu.CompilerParams(vmem_limit_bytes=8 * 1024 * 1024),
        name="small_last" if last else "small",
    )(core, mine, other, vec, res, sol, image)


def body(groups, crossed, bits, core_bit, count, cols, right_side, diag_vals, tiles, col_ids):
    rows, nbr, blk, _ = tiles.shape
    me = lax.axis_index("row") * cols + lax.axis_index("col")
    core = ((me & core_bit) != 0).astype(jnp.int32)[None]
    ids = col_ids.reshape(-1)
    slots = slot_of(me, ids // rows, groups, crossed, core_bit) * rows + ids % rows
    slots = jnp.concatenate([slots, core])
    diag = diag_vals[None, :]
    sol = jnp.zeros_like(right_side)
    rounded, res = round_blocks(right_side, rows)
    vec = res
    for step in range(ITERS):
        last = step + 1 == ITERS
        pieces = gather_of(rounded, groups, crossed, core_bit, count)
        image, keep, give = apply_matrix(slots, pieces, tiles, vec, res, diag)
        mine = keep + xor_permute(give, core_bit, count)
        for mask in bits:
            mine = mine + xor_permute(mine, mask, count)
        other = xor_permute(mine, core_bit, count)
        outs = solve_step(last, rows, core, mine, other, vec, res, sol, image)
        if last:
            sol, res = outs
        else:
            sol, res, vec, rounded = outs
    return (sol, res)


def solution(mesh):
    placed = (
        P(None, ("row", "col")),
        P(("row", "col")),
        P(("row", "col"), None, None, None),
        P(("row", "col"), None),
    )
    count = mesh.shape["row"] * mesh.shape["col"]
    cols = mesh.shape["col"]
    bits = [1 << i for i in range(1, count.bit_length() - 1)]
    crossed, rest = bits[:2], bits[2:]
    major = [b for b in rest if b >= cols]
    minor = [b for b in rest if b < cols]
    groups = [part[i : i + 2] for part in (major, minor) for i in range(0, len(part), 2)]
    return jax.shard_map(
        functools.partial(body, groups, crossed, bits, 1, count, cols),
        mesh=mesh,
        in_specs=placed,
        out_specs=(P(None, ("row", "col")), P(None, ("row", "col"))),
        check_vma=False,
    )
```

```python
import functools

import jax
import jax.numpy as jnp
from jax import lax
from jax.experimental import pallas as pl
from jax.experimental.pallas import tpu as pltpu
from jax.sharding import PartitionSpec as P

ITERS = 4
AXES = ("row", "col")
HIGH = lax.Precision.HIGHEST


def nn(left, right):
    return lax.dot_general(
        left, right, (((1,), (0,)), ((), ())), precision=HIGH, preferred_element_type=jnp.float32
    )


def nt(left, right):
    return lax.dot_general(
        left, right, (((1,), (1,)), ((), ())), precision=HIGH, preferred_element_type=jnp.float32
    )


def xor_permute(val, mask, count):
    return lax.ppermute(val, AXES, [(i, i ^ mask) for i in range(count)])


def spread(val, masks, count):
    partners = [0]
    for mask in masks:
        partners = partners + [p ^ mask for p in partners]
    return [val] + [xor_permute(val, p, count) for p in partners[1:]]


def crossed_permute(val, even, odd, core, count):
    return lax.ppermute(val, AXES, [(i, i ^ (odd if i & core else even)) for i in range(count)])


def gather_of(val, groups, crossed, core, count):
    for masks in groups[:-1]:
        val = jnp.concatenate(spread(val, masks, count), axis=0)
    parts = spread(val, groups[-1], count)
    half = len(parts) // 2
    halves = [jnp.concatenate(parts[:half], axis=0), jnp.concatenate(parts[half:], axis=0)]
    one, two = crossed
    near = [crossed_permute(part, one, two, core, count) for part in halves]
    far = [crossed_permute(part, two, one, core, count) for part in halves]
    both = [crossed_permute(part, two, one, core, count) for part in near]
    pieces = halves + near + far + both
    return pieces + [xor_permute(piece, core, count) for piece in pieces]


def slot_of(me, other, groups, crossed, core):
    diff = me ^ other
    slot = jnp.zeros_like(diff)
    place = 1
    for masks in groups:
        for mask in masks:
            slot = slot + jnp.where((diff & mask) != 0, place, 0)
            place *= 2
    one, two = crossed
    at_one = (other & core) != 0
    first = jnp.where(at_one, diff & two, diff & one) != 0
    second = jnp.where(at_one, diff & one, diff & two) != 0
    slot = slot + jnp.where(first, place, 0) + jnp.where(second, 2 * place, 0)
    return slot + jnp.where((diff & core) != 0, 4 * place, 0)


def matrix_kernel(rows, nbr, blk, count, slots, tiles, vec, res, diag, *refs):
    pieces, (image, keep, give, whole) = refs[:count], refs[count:]
    coef = 1.0 / (nbr * blk)
    first = 0
    for piece in pieces:
        whole[first : first + piece.shape[0]] = piece[...]
        first += piece.shape[0]
    n = vec.shape[0]
    for row in range(rows):
        acc = jnp.zeros((n, blk), jnp.float32)
        for k in range(nbr):
            spot = row * nbr + k
            acc = acc + lax.dot_general(
                whole[slots[spot]],
                tiles[row, k],
                (((1,), (1,)), ((), ())),
                preferred_element_type=jnp.float32,
            )
        cols = pl.ds(row * blk, blk)
        image[:, cols] = diag[:, cols] * vec[:, cols] + coef * acc
    img = image[...]
    old = res[...]
    both = nt(jnp.concatenate([old, img], axis=0), jnp.concatenate([old, img], axis=0))
    curv = nt(vec[...], img)
    first = jnp.concatenate([both[0:n, 0:n], curv], axis=1)
    second = both[:, n : 2 * n]
    second = jnp.concatenate([second[0:n], second[n : 2 * n]], axis=1)
    core = slots[rows * nbr]
    keep[...] = jnp.where(core == 0, first, second)
    give[...] = jnp.where(core == 0, second, first)


def round_kernel(source, target, same):
    blk = target.shape[2]
    for row in range(target.shape[0]):
        target[row] = source[:, row * blk : (row + 1) * blk].astype(jnp.bfloat16)
    same[...] = source[...]


def round_blocks(source, rows):
    n, width = source.shape
    vmem = pl.BlockSpec(memory_space=pltpu.VMEM)
    return pl.pallas_call(
        round_kernel,
        out_shape=(
            jax.ShapeDtypeStruct((rows, n, width // rows), jnp.bfloat16),
            jax.ShapeDtypeStruct(source.shape, source.dtype),
        ),
        in_specs=[vmem],
        out_specs=(vmem, vmem),
        compiler_params=pltpu.CompilerParams(vmem_limit_bytes=4 * 1024 * 1024),
        name="round",
    )(source)


def apply_matrix(slots, pieces, tiles, vec, res, diag):
    rows, nbr, blk, _ = tiles.shape
    n = vec.shape[0]
    vmem = pl.BlockSpec(memory_space=pltpu.VMEM)
    half = jax.ShapeDtypeStruct((n, 2 * n), jnp.float32)
    blocks = sum(piece.shape[0] for piece in pieces)
    grant = 2 * blocks * n * blk * 2 + tiles.size * 2 + 2 * 1024 * 1024
    return pl.pallas_call(
        functools.partial(matrix_kernel, rows, nbr, blk, len(pieces)),
        out_shape=(jax.ShapeDtypeStruct(vec.shape, jnp.float32), half, half),
        in_specs=[pl.BlockSpec(memory_space=pltpu.SMEM), vmem, vmem, vmem, vmem]
        + [vmem] * len(pieces),
        out_specs=(vmem, vmem, vmem),
        scratch_shapes=[
            pltpu.VMEM((blocks, n, blk), tiles.dtype),
        ],
        compiler_params=pltpu.CompilerParams(vmem_limit_bytes=grant),
        name="matrix",
    )(slots, tiles, vec, res, diag, *pieces)


def invert_pair(mats, n):
    size = 8
    width = 2 * n
    lanes = lax.broadcasted_iota(jnp.int32, (size, width), 1)
    rows = lax.broadcasted_iota(jnp.int32, (size, width), 0)
    left = lanes < n
    place = jnp.where(left, lanes, lanes - n)
    line_place = place[0:1, :]
    blocks = [mats[i : i + size, :] for i in range(0, n, size)]
    for at in range(n // size):
        base = at * size
        spread_cols = [
            [
                jnp.where(
                    left,
                    jnp.broadcast_to(block[:, base + i : base + i + 1], (size, width)),
                    jnp.broadcast_to(block[:, n + base + i : n + base + i + 1], (size, width)),
                )
                for i in range(size)
            ]
            for block in blocks
        ]
        own = spread_cols[at]
        inside = (line_place >= base) & (line_place < base + size)
        lines = [
            jnp.where(line_place == base + i, 1.0, jnp.where(inside, 0.0, blocks[at][i : i + 1, :]))
            for i in range(size)
        ]
        upper = [[own[k][i : i + 1, :] if k >= i else None for k in range(size)] for i in range(size)]
        for i in range(size):
            inv = 1.0 / upper[i][i]
            for m in range(i + 1, size):
                factor = upper[i][m] * inv
                for k in range(m, size):
                    upper[m][k] = upper[m][k] - factor * upper[i][k]
                lines[m] = lines[m] - factor * lines[i]
            upper[i][i] = inv
        for i in reversed(range(size)):
            for k in range(i + 1, size):
                lines[i] = lines[i] - upper[i][k] * lines[k]
            lines[i] = lines[i] * upper[i][i]
        within = (place >= base) & (place < base + size)
        solved = jnp.broadcast_to(lines[0], (size, width))
        for i in range(1, size):
            solved = jnp.where(rows == i, jnp.broadcast_to(lines[i], (size, width)), solved)
        for q, block in enumerate(blocks):
            if q == at:
                continue
            kept = jnp.where(within, 0.0, block)
            for i in range(size):
                kept = kept - spread_cols[q][i] * lines[i]
            blocks[q] = kept
        blocks[at] = solved
    return jnp.concatenate(blocks, axis=0)


def solve_kernel(last, core, mine, other, vec, res, sol, image, *outs):
    n = vec.shape[0]
    at_zero = core[0] == 0
    first = jnp.where(at_zero, mine[...], other[...])
    gram, curv = first[:, 0:n], first[:, n : 2 * n]
    inverses = invert_pair(jnp.concatenate([curv, gram], axis=1), n)
    alpha_t = nn(gram, inverses[:, 0:n])
    old = vec[...]
    new = res[...] - nn(alpha_t, image[...])
    outs[0][...] = sol[...] + nn(alpha_t, old)
    outs[1][...] = new
    if not last:
        second = jnp.where(at_zero, other[...], mine[...])
        cross, square = second[:, 0:n], second[:, n : 2 * n]
        mixed = nt(cross, alpha_t)
        gram_new = gram - mixed + nn(alpha_t, nt(square, alpha_t) - cross.T)
        beta_t = nn(gram_new, inverses[:, n : 2 * n])
        step = new + nn(beta_t, old)
        outs[2][...] = step
        blk = outs[3].shape[2]
        for row in range(outs[3].shape[0]):
            outs[3][row] = step[:, row * blk : (row + 1) * blk].astype(jnp.bfloat16)


def solve_step(last, rows, core, mine, other, vec, res, sol, image):
    shape = jax.ShapeDtypeStruct(vec.shape, jnp.float32)
    n, width = vec.shape
    space = pl.BlockSpec(memory_space=pltpu.VMEM)
    outs = [shape, shape]
    if not last:
        outs += [shape, jax.ShapeDtypeStruct((rows, n, width // rows), jnp.bfloat16)]
    return pl.pallas_call(
        functools.partial(solve_kernel, last),
        out_shape=tuple(outs),
        in_specs=[pl.BlockSpec(memory_space=pltpu.SMEM)] + [space] * 6,
        out_specs=tuple([space] * len(outs)),
        compiler_params=pltpu.CompilerParams(vmem_limit_bytes=8 * 1024 * 1024),
        name="small_last" if last else "small",
    )(core, mine, other, vec, res, sol, image)


def body(groups, crossed, stages, core_bit, count, cols, right_side, diag_vals, tiles, col_ids):
    rows, nbr, blk, _ = tiles.shape
    me = lax.axis_index("row") * cols + lax.axis_index("col")
    core = ((me & core_bit) != 0).astype(jnp.int32)[None]
    ids = col_ids.reshape(-1)
    slots = slot_of(me, ids // rows, groups, crossed, core_bit) * rows + ids % rows
    slots = jnp.concatenate([slots, core])
    diag = diag_vals[None, :]
    sol = jnp.zeros_like(right_side)
    rounded, res = round_blocks(right_side, rows)
    vec = res
    for step in range(ITERS):
        last = step + 1 == ITERS
        pieces = gather_of(rounded, groups, crossed, core_bit, count)
        image, keep, give = apply_matrix(slots, pieces, tiles, vec, res, diag)
        mine = keep + xor_permute(give, core_bit, count)
        for even, odd in stages:
            mine = mine + crossed_permute(mine, even, odd, core_bit, count)
        other = xor_permute(mine, core_bit, count)
        outs = solve_step(last, rows, core, mine, other, vec, res, sol, image)
        if last:
            sol, res = outs
        else:
            sol, res, vec, rounded = outs
    return (sol, res)


def solution(mesh):
    placed = (
        P(None, ("row", "col")),
        P(("row", "col")),
        P(("row", "col"), None, None, None),
        P(("row", "col"), None),
    )
    count = mesh.shape["row"] * mesh.shape["col"]
    cols = mesh.shape["col"]
    bits = [1 << i for i in range(1, count.bit_length() - 1)]
    crossed, rest = bits[:2], bits[2:]
    stages = []
    for i in range(0, len(bits), 2):
        pair = bits[i : i + 2]
        stages += [(pair[0], pair[-1]), (pair[-1], pair[0])][: len(pair)]
    major = [b for b in rest if b >= cols]
    minor = [b for b in rest if b < cols]
    groups = [part[i : i + 2] for part in (major, minor) for i in range(0, len(part), 2)]
    return jax.shard_map(
        functools.partial(body, groups, crossed, stages, 1, count, cols),
        mesh=mesh,
        in_specs=placed,
        out_specs=(P(None, ("row", "col")), P(None, ("row", "col"))),
        check_vma=False,
    )
```

```python
import functools

import jax
import jax.numpy as jnp
from jax import lax
from jax.experimental import pallas as pl
from jax.experimental.pallas import tpu as pltpu
from jax.sharding import PartitionSpec as P

ITERS = 4
AXES = ("row", "col")
HIGH = lax.Precision.HIGHEST


def nn(left, right):
    return lax.dot_general(
        left, right, (((1,), (0,)), ((), ())), precision=HIGH, preferred_element_type=jnp.float32
    )


def nt(left, right):
    return lax.dot_general(
        left, right, (((1,), (1,)), ((), ())), precision=HIGH, preferred_element_type=jnp.float32
    )


def xor_permute(val, mask, count):
    return lax.ppermute(val, AXES, [(i, i ^ mask) for i in range(count)])


def spread(val, masks, count):
    partners = [0]
    for mask in masks:
        partners = partners + [p ^ mask for p in partners]
    return [val] + [xor_permute(val, p, count) for p in partners[1:]]


def crossed_permute(val, even, odd, core, count):
    return lax.ppermute(val, AXES, [(i, i ^ (odd if i & core else even)) for i in range(count)])


def gather_of(val, groups, crossed, core, count):
    for masks in groups[:-1]:
        val = jnp.concatenate(spread(val, masks, count), axis=0)
    parts = spread(val, groups[-1], count)
    half = len(parts) // 2
    halves = [jnp.concatenate(parts[:half], axis=0), jnp.concatenate(parts[half:], axis=0)]
    one, two = crossed
    near = [crossed_permute(part, one, two, core, count) for part in halves]
    far = [crossed_permute(part, two, one, core, count) for part in halves]
    both = [crossed_permute(part, two, one, core, count) for part in near]
    pieces = halves + near + far + both
    return pieces + [xor_permute(piece, core, count) for piece in pieces]


def slot_of(me, other, groups, crossed, core):
    diff = me ^ other
    slot = jnp.zeros_like(diff)
    place = 1
    for masks in groups:
        for mask in masks:
            slot = slot + jnp.where((diff & mask) != 0, place, 0)
            place *= 2
    one, two = crossed
    at_one = (other & core) != 0
    first = jnp.where(at_one, diff & two, diff & one) != 0
    second = jnp.where(at_one, diff & one, diff & two) != 0
    slot = slot + jnp.where(first, place, 0) + jnp.where(second, 2 * place, 0)
    return slot + jnp.where((diff & core) != 0, 4 * place, 0)


def matrix_kernel(rows, nbr, blk, count, slots, tiles, vec, res, diag, *refs):
    pieces, (image, keep, give, whole) = refs[:count], refs[count:]
    coef = 1.0 / (nbr * blk)
    first = 0
    for piece in pieces:
        whole[first : first + piece.shape[0]] = piece[...]
        first += piece.shape[0]
    n = vec.shape[0]
    for row in range(rows):
        acc = jnp.zeros((n, blk), jnp.float32)
        for k in range(nbr):
            spot = row * nbr + k
            acc = acc + lax.dot_general(
                whole[slots[spot]],
                tiles[row, k],
                (((1,), (1,)), ((), ())),
                preferred_element_type=jnp.float32,
            )
        cols = pl.ds(row * blk, blk)
        image[:, cols] = diag[:, cols] * vec[:, cols] + coef * acc
    img = image[...]
    old = res[...]
    both = nt(jnp.concatenate([old, img], axis=0), jnp.concatenate([old, img], axis=0))
    curv = nt(vec[...], img)
    first = jnp.concatenate([both[0:n, 0:n], curv], axis=1)
    second = both[:, n : 2 * n]
    second = jnp.concatenate([second[0:n], second[n : 2 * n]], axis=1)
    core = slots[rows * nbr]
    keep[...] = jnp.where(core == 0, first, second)
    give[...] = jnp.where(core == 0, second, first)


def round_kernel(source, target, same):
    blk = target.shape[2]
    for row in range(target.shape[0]):
        target[row] = source[:, row * blk : (row + 1) * blk].astype(jnp.bfloat16)
    same[...] = source[...]


def round_blocks(source, rows):
    n, width = source.shape
    vmem = pl.BlockSpec(memory_space=pltpu.VMEM)
    return pl.pallas_call(
        round_kernel,
        out_shape=(
            jax.ShapeDtypeStruct((rows, n, width // rows), jnp.bfloat16),
            jax.ShapeDtypeStruct(source.shape, source.dtype),
        ),
        in_specs=[vmem],
        out_specs=(vmem, vmem),
        compiler_params=pltpu.CompilerParams(vmem_limit_bytes=4 * 1024 * 1024),
        name="round",
    )(source)


def apply_matrix(slots, pieces, tiles, vec, res, diag):
    rows, nbr, blk, _ = tiles.shape
    n = vec.shape[0]
    vmem = pl.BlockSpec(memory_space=pltpu.VMEM)
    half = jax.ShapeDtypeStruct((n, 2 * n), jnp.float32)
    blocks = sum(piece.shape[0] for piece in pieces)
    grant = 2 * blocks * n * blk * 2 + tiles.size * 2 + 2 * 1024 * 1024
    return pl.pallas_call(
        functools.partial(matrix_kernel, rows, nbr, blk, len(pieces)),
        out_shape=(jax.ShapeDtypeStruct(vec.shape, jnp.float32), half, half),
        in_specs=[pl.BlockSpec(memory_space=pltpu.SMEM), vmem, vmem, vmem, vmem]
        + [vmem] * len(pieces),
        out_specs=(vmem, vmem, vmem),
        scratch_shapes=[
            pltpu.VMEM((blocks, n, blk), tiles.dtype),
        ],
        compiler_params=pltpu.CompilerParams(vmem_limit_bytes=grant),
        name="matrix",
    )(slots, tiles, vec, res, diag, *pieces)


def invert_pair(mats, n):
    size = 8
    width = 2 * n
    lanes = lax.broadcasted_iota(jnp.int32, (size, width), 1)
    rows = lax.broadcasted_iota(jnp.int32, (size, width), 0)
    left = lanes < n
    place = jnp.where(left, lanes, lanes - n)
    line_place = place[0:1, :]
    blocks = [mats[i : i + size, :] for i in range(0, n, size)]
    for at in range(n // size):
        base = at * size
        spread_cols = [
            [
                jnp.where(
                    left,
                    jnp.broadcast_to(block[:, base + i : base + i + 1], (size, width)),
                    jnp.broadcast_to(block[:, n + base + i : n + base + i + 1], (size, width)),
                )
                for i in range(size)
            ]
            for block in blocks
        ]
        own = spread_cols[at]
        inside = (line_place >= base) & (line_place < base + size)
        lines = [
            jnp.where(line_place == base + i, 1.0, jnp.where(inside, 0.0, blocks[at][i : i + 1, :]))
            for i in range(size)
        ]
        upper = [[own[k][i : i + 1, :] if k >= i else None for k in range(size)] for i in range(size)]
        for i in range(size):
            inv = 1.0 / upper[i][i]
            for m in range(i + 1, size):
                factor = upper[i][m] * inv
                for k in range(m, size):
                    upper[m][k] = upper[m][k] - factor * upper[i][k]
                lines[m] = lines[m] - factor * lines[i]
            upper[i][i] = inv
        for i in reversed(range(size)):
            for k in range(i + 1, size):
                lines[i] = lines[i] - upper[i][k] * lines[k]
            lines[i] = lines[i] * upper[i][i]
        within = (place >= base) & (place < base + size)
        solved = jnp.broadcast_to(lines[0], (size, width))
        for i in range(1, size):
            solved = jnp.where(rows == i, jnp.broadcast_to(lines[i], (size, width)), solved)
        for q, block in enumerate(blocks):
            if q == at:
                continue
            kept = jnp.where(within, 0.0, block)
            for i in range(size):
                kept = kept - spread_cols[q][i] * lines[i]
            blocks[q] = kept
        blocks[at] = solved
    return jnp.concatenate(blocks, axis=0)


def solve_kernel(last, core, mine, other, vec, res, sol, image, *outs):
    n = vec.shape[0]
    at_zero = core[0] == 0
    first = jnp.where(at_zero, mine[...], other[...])
    gram, curv = first[:, 0:n], first[:, n : 2 * n]
    inverses = invert_pair(jnp.concatenate([curv, gram], axis=1), n)
    alpha_t = nn(gram, inverses[:, 0:n])
    old = vec[...]
    new = res[...] - nn(alpha_t, image[...])
    outs[0][...] = sol[...] + nn(alpha_t, old)
    outs[1][...] = new
    if not last:
        second = jnp.where(at_zero, other[...], mine[...])
        cross, square = second[:, 0:n], second[:, n : 2 * n]
        mixed = nt(cross, alpha_t)
        gram_new = gram - mixed + nn(alpha_t, nt(square, alpha_t) - cross.T)
        beta_t = nn(gram_new, inverses[:, n : 2 * n])
        step = new + nn(beta_t, old)
        outs[2][...] = step
        blk = outs[3].shape[2]
        for row in range(outs[3].shape[0]):
            outs[3][row] = step[:, row * blk : (row + 1) * blk].astype(jnp.bfloat16)


def solve_step(last, rows, core, mine, other, vec, res, sol, image):
    shape = jax.ShapeDtypeStruct(vec.shape, jnp.float32)
    n, width = vec.shape
    space = pl.BlockSpec(memory_space=pltpu.VMEM)
    outs = [shape, shape]
    if not last:
        outs += [shape, jax.ShapeDtypeStruct((rows, n, width // rows), jnp.bfloat16)]
    return pl.pallas_call(
        functools.partial(solve_kernel, last),
        out_shape=tuple(outs),
        in_specs=[pl.BlockSpec(memory_space=pltpu.SMEM)] + [space] * 6,
        out_specs=tuple([space] * len(outs)),
        compiler_params=pltpu.CompilerParams(vmem_limit_bytes=8 * 1024 * 1024),
        name="small_last" if last else "small",
    )(core, mine, other, vec, res, sol, image)


def body(groups, crossed, stages, core_bit, count, cols, right_side, diag_vals, tiles, col_ids):
    rows, nbr, blk, _ = tiles.shape
    me = lax.axis_index("row") * cols + lax.axis_index("col")
    core = ((me & core_bit) != 0).astype(jnp.int32)[None]
    ids = col_ids.reshape(-1)
    slots = slot_of(me, ids // rows, groups, crossed, core_bit) * rows + ids % rows
    slots = jnp.concatenate([slots, core])
    diag = diag_vals[None, :]
    sol = jnp.zeros_like(right_side)
    rounded, res = round_blocks(right_side, rows)
    vec = res
    for step in range(ITERS):
        last = step + 1 == ITERS
        pieces = gather_of(rounded, groups, crossed, core_bit, count)
        image, keep, give = apply_matrix(slots, pieces, tiles, vec, res, diag)
        mine = keep + xor_permute(give, core_bit, count)
        for masks in stages:
            terms = spread(mine, masks, count)
            while len(terms) > 1:
                terms = [left + right for left, right in zip(terms[0::2], terms[1::2])]
            mine = terms[0]
        other = xor_permute(mine, core_bit, count)
        outs = solve_step(last, rows, core, mine, other, vec, res, sol, image)
        if last:
            sol, res = outs
        else:
            sol, res, vec, rounded = outs
    return (sol, res)


def solution(mesh):
    placed = (
        P(None, ("row", "col")),
        P(("row", "col")),
        P(("row", "col"), None, None, None),
        P(("row", "col"), None),
    )
    count = mesh.shape["row"] * mesh.shape["col"]
    cols = mesh.shape["col"]
    bits = [1 << i for i in range(1, count.bit_length() - 1)]
    crossed, rest = bits[:2], bits[2:]
    stages = [bits[i : i + 2] for i in range(0, len(bits), 2)]
    major = [b for b in rest if b >= cols]
    minor = [b for b in rest if b < cols]
    groups = [part[i : i + 2] for part in (major, minor) for i in range(0, len(part), 2)]
    return jax.shard_map(
        functools.partial(body, groups, crossed, stages, 1, count, cols),
        mesh=mesh,
        in_specs=placed,
        out_specs=(P(None, ("row", "col")), P(None, ("row", "col"))),
        check_vma=False,
    )
```

```python
import functools

import jax
import jax.numpy as jnp
from jax import lax
from jax.experimental import pallas as pl
from jax.experimental.pallas import tpu as pltpu
from jax.sharding import PartitionSpec as P

ITERS = 4
AXES = ("row", "col")
HIGH = lax.Precision.HIGHEST


def nn(left, right):
    return lax.dot_general(
        left, right, (((1,), (0,)), ((), ())), precision=HIGH, preferred_element_type=jnp.float32
    )


def nt(left, right):
    return lax.dot_general(
        left, right, (((1,), (1,)), ((), ())), precision=HIGH, preferred_element_type=jnp.float32
    )


def xor_permute(val, mask, count):
    return lax.ppermute(val, AXES, [(i, i ^ mask) for i in range(count)])


def spread(val, masks, count):
    partners = [0]
    for mask in masks:
        partners = partners + [p ^ mask for p in partners]
    return [val] + [xor_permute(val, p, count) for p in partners[1:]]


def crossed_permute(val, even, odd, core, count):
    return lax.ppermute(val, AXES, [(i, i ^ (odd if i & core else even)) for i in range(count)])


def gather_of(val, groups, crossed, core, count):
    for masks in groups[:-1]:
        val = jnp.concatenate(spread(val, masks, count), axis=0)
    parts = spread(val, groups[-1], count)
    half = len(parts) // 2
    halves = [jnp.concatenate(parts[:half], axis=0), jnp.concatenate(parts[half:], axis=0)]
    one, two = crossed
    near = [crossed_permute(part, one, two, core, count) for part in halves]
    far = [crossed_permute(part, two, one, core, count) for part in halves]
    both = [crossed_permute(part, two, one, core, count) for part in near]
    pieces = halves + near + far + both
    return pieces


def slot_of(me, other, groups, crossed, core):
    diff = me ^ other
    slot = jnp.zeros_like(diff)
    place = 1
    for masks in groups:
        for mask in masks:
            slot = slot + jnp.where((diff & mask) != 0, place, 0)
            place *= 2
    one, two = crossed
    at_one = (other & core) != 0
    first = jnp.where(at_one, diff & two, diff & one) != 0
    second = jnp.where(at_one, diff & one, diff & two) != 0
    slot = slot + jnp.where(first, place, 0) + jnp.where(second, 2 * place, 0)
    return slot + jnp.where((diff & core) != 0, 4 * place, 0)


def matrix_kernel(rows, nbr, blk, count, last, slots, tiles, vec, res, diag, *refs):
    pieces, (image, keep, give, whole) = refs[:count], refs[count:]
    coef = 1.0 / (nbr * blk)
    at = 0
    for piece in pieces:
        whole[at : at + piece.shape[0]] = piece[...]
        at += piece.shape[0]
    n = vec.shape[0]
    for row in range(rows):
        acc = jnp.zeros((n, blk), jnp.float32)
        for k in range(nbr):
            spot = row * nbr + k
            acc = acc + lax.dot_general(
                whole[slots[spot]],
                tiles[row, k],
                (((1,), (1,)), ((), ())),
                preferred_element_type=jnp.float32,
            )
        cols = pl.ds(row * blk, blk)
        image[:, cols] = diag[:, cols] * vec[:, cols] + coef * acc
    img = image[...]
    old = res[...]
    curv = nt(vec[...], img)
    core = slots[rows * nbr]
    if last:
        both = jnp.concatenate([nt(old, old), curv], axis=1)
        first, second = both[0 : n // 2], both[n // 2 : n]
    else:
        both = nt(jnp.concatenate([old, img], axis=0), jnp.concatenate([old, img], axis=0))
        first = jnp.concatenate([both[0:n, 0:n], curv], axis=1)
        second = jnp.concatenate([both[0:n, n : 2 * n], both[n : 2 * n, n : 2 * n]], axis=1)
    keep[...] = jnp.where(core == 0, first, second)
    give[...] = jnp.where(core == 0, second, first)


def round_kernel(source, target, same):
    blk = target.shape[2]
    for row in range(target.shape[0]):
        target[row] = source[:, row * blk : (row + 1) * blk].astype(jnp.bfloat16)
    same[...] = source[...]


def round_blocks(source, rows):
    n, width = source.shape
    vmem = pl.BlockSpec(memory_space=pltpu.VMEM)
    return pl.pallas_call(
        round_kernel,
        out_shape=(
            jax.ShapeDtypeStruct((rows, n, width // rows), jnp.bfloat16),
            jax.ShapeDtypeStruct(source.shape, source.dtype),
        ),
        in_specs=[vmem],
        out_specs=(vmem, vmem),
        compiler_params=pltpu.CompilerParams(vmem_limit_bytes=4 * 1024 * 1024),
        name="round",
    )(source)


def load_kernel(parts, source, diag, after, target, diag_target, token, sems):
    del after
    rows = source.shape[0] // parts
    copies = [pltpu.make_async_copy(diag, diag_target, sems.at[parts])]
    for part in range(parts):
        span = pl.ds(part * rows, rows)
        copies.append(pltpu.make_async_copy(source.at[span], target.at[span], sems.at[part]))
    for copy in copies:
        copy.start()
    token[...] = jnp.zeros_like(token)
    for copy in copies:
        copy.wait()


def load(source, diag, after):
    anywhere = pl.BlockSpec(memory_space=pl.ANY)
    vmem = pl.BlockSpec(memory_space=pltpu.VMEM)
    parts = source.shape[0]
    return pl.pallas_call(
        functools.partial(load_kernel, parts),
        out_shape=(
            jax.ShapeDtypeStruct(source.shape, source.dtype),
            jax.ShapeDtypeStruct(diag.shape, diag.dtype),
            jax.ShapeDtypeStruct((8, 128), jnp.float32),
        ),
        in_specs=[anywhere] * 3,
        out_specs=(vmem, vmem, vmem),
        scratch_shapes=[pltpu.SemaphoreType.DMA((parts + 1,))],
        compiler_params=pltpu.CompilerParams(vmem_limit_bytes=6 * 1024 * 1024),
        name="load",
    )(
        pltpu.with_memory_space_constraint(source, pltpu.HBM),
        pltpu.with_memory_space_constraint(diag, pltpu.HBM),
        after,
    )


def apply_matrix(last, slots, pieces, tiles, vec, res, diag):
    rows, nbr, blk, _ = tiles.shape
    n = vec.shape[0]
    vmem = pl.BlockSpec(memory_space=pltpu.VMEM)
    blocks = sum(piece.shape[0] for piece in pieces)
    grant = 2 * blocks * n * blk * 2 + tiles.size * 2 + 2 * 1024 * 1024
    half = jax.ShapeDtypeStruct((n // 2 if last else n, 2 * n), jnp.float32)
    outs = [jax.ShapeDtypeStruct(vec.shape, jnp.float32), half, half]
    scratch = [pltpu.VMEM((blocks, n, blk), tiles.dtype)]
    return pl.pallas_call(
        functools.partial(matrix_kernel, rows, nbr, blk, len(pieces), last),
        out_shape=tuple(outs),
        in_specs=[pl.BlockSpec(memory_space=pltpu.SMEM), vmem, vmem, vmem, vmem]
        + [vmem] * len(pieces),
        out_specs=tuple([vmem] * len(outs)),
        scratch_shapes=scratch,
        compiler_params=pltpu.CompilerParams(vmem_limit_bytes=grant),
        name="matrix",
    )(slots, tiles, vec, res, diag, *pieces)


def invert_pair(mats, n):
    size = 8
    width = 2 * n
    lanes = lax.broadcasted_iota(jnp.int32, (size, width), 1)
    rows = lax.broadcasted_iota(jnp.int32, (size, width), 0)
    left = lanes < n
    place = jnp.where(left, lanes, lanes - n)
    line_place = place[0:1, :]
    blocks = [mats[i : i + size, :] for i in range(0, n, size)]
    for at in range(n // size):
        base = at * size
        spread_cols = [
            [
                jnp.where(
                    left,
                    jnp.broadcast_to(block[:, base + i : base + i + 1], (size, width)),
                    jnp.broadcast_to(block[:, n + base + i : n + base + i + 1], (size, width)),
                )
                for i in range(size)
            ]
            for block in blocks
        ]
        own = spread_cols[at]
        inside = (line_place >= base) & (line_place < base + size)
        lines = [
            jnp.where(line_place == base + i, 1.0, jnp.where(inside, 0.0, blocks[at][i : i + 1, :]))
            for i in range(size)
        ]
        upper = [[own[k][i : i + 1, :] if k >= i else None for k in range(size)] for i in range(size)]
        for i in range(size):
            inv = 1.0 / upper[i][i]
            for m in range(i + 1, size):
                factor = upper[i][m] * inv
                for k in range(m, size):
                    upper[m][k] = upper[m][k] - factor * upper[i][k]
                lines[m] = lines[m] - factor * lines[i]
            upper[i][i] = inv
        for i in reversed(range(size)):
            for k in range(i + 1, size):
                lines[i] = lines[i] - upper[i][k] * lines[k]
            lines[i] = lines[i] * upper[i][i]
        within = (place >= base) & (place < base + size)
        solved = jnp.broadcast_to(lines[0], (size, width))
        for i in range(1, size):
            solved = jnp.where(rows == i, jnp.broadcast_to(lines[i], (size, width)), solved)
        for q, block in enumerate(blocks):
            if q == at:
                continue
            kept = jnp.where(within, 0.0, block)
            for i in range(size):
                kept = kept - spread_cols[q][i] * lines[i]
            blocks[q] = kept
        blocks[at] = solved
    return jnp.concatenate(blocks, axis=0)


def solve_kernel(last, core, mine, other, vec, res, sol, image, *outs):
    n = vec.shape[0]
    at_zero = core[0] == 0
    first = jnp.where(at_zero, mine[...], other[...])
    if last:
        first = jnp.concatenate([first, jnp.where(at_zero, other[...], mine[...])], axis=0)
    gram, curv = first[:, 0:n], first[:, n : 2 * n]
    inverses = invert_pair(jnp.concatenate([curv, gram], axis=1), n)
    alpha_t = nn(gram, inverses[:, 0:n])
    old = vec[...]
    new = res[...] - nn(alpha_t, image[...])
    outs[0][...] = sol[...] + nn(alpha_t, old)
    outs[1][...] = new
    if not last:
        second = jnp.where(at_zero, other[...], mine[...])
        cross, square = second[:, 0:n], second[:, n : 2 * n]
        mixed = nt(cross, alpha_t)
        gram_new = gram - mixed + nn(alpha_t, nt(square, alpha_t) - cross.T)
        beta_t = nn(gram_new, inverses[:, n : 2 * n])
        step = new + nn(beta_t, old)
        outs[2][...] = step
        blk = outs[3].shape[2]
        for row in range(outs[3].shape[0]):
            outs[3][row] = step[:, row * blk : (row + 1) * blk].astype(jnp.bfloat16)


def solve_step(last, rows, core, mine, other, vec, res, sol, image):
    shape = jax.ShapeDtypeStruct(vec.shape, jnp.float32)
    n, width = vec.shape
    space = pl.BlockSpec(memory_space=pltpu.VMEM)
    outs = [shape, shape]
    if not last:
        outs += [shape, jax.ShapeDtypeStruct((rows, n, width // rows), jnp.bfloat16)]
    return pl.pallas_call(
        functools.partial(solve_kernel, last),
        out_shape=tuple(outs),
        in_specs=[pl.BlockSpec(memory_space=pltpu.SMEM)] + [space] * 6,
        out_specs=tuple([space] * len(outs)),
        compiler_params=pltpu.CompilerParams(vmem_limit_bytes=8 * 1024 * 1024),
        name="small_last" if last else "small",
    )(core, mine, other, vec, res, sol, image)


def body(groups, crossed, stages, core_bit, count, cols, right_side, diag_vals, tiles, col_ids):
    rows, nbr, blk, _ = tiles.shape
    me = lax.axis_index("row") * cols + lax.axis_index("col")
    core = ((me & core_bit) != 0).astype(jnp.int32)[None]
    ids = col_ids.reshape(-1)
    slots = slot_of(me, ids // rows, groups, crossed, core_bit) * rows + ids % rows
    slots = jnp.concatenate([slots, core])
    diag = diag_vals[None, :]
    sol = jnp.zeros_like(right_side)
    rounded, res = round_blocks(right_side, rows)
    vec = res
    for step in range(ITERS):
        last = step + 1 == ITERS
        pieces = gather_of(rounded, groups, crossed, core_bit, count)
        if step == 0:
            tiles, diag, token = load(tiles, diag, pieces[3])
            pieces[5], _ = lax.optimization_barrier((pieces[5], token))
        pieces += [xor_permute(piece, core_bit, count) for piece in pieces]
        image, keep, give = apply_matrix(last, slots, pieces, tiles, vec, res, diag)
        mine = keep + xor_permute(give, core_bit, count)
        for masks in stages:
            terms = spread(mine, masks, count)
            while len(terms) > 1:
                terms = [left + right for left, right in zip(terms[0::2], terms[1::2])]
            mine = terms[0]
        other = xor_permute(mine, core_bit, count)
        outs = solve_step(last, rows, core, mine, other, vec, res, sol, image)
        if last:
            sol, res = outs
        else:
            sol, res, vec, rounded = outs
    return (sol, res)


def solution(mesh):
    placed = (
        P(None, ("row", "col")),
        P(("row", "col")),
        P(("row", "col"), None, None, None),
        P(("row", "col"), None),
    )
    count = mesh.shape["row"] * mesh.shape["col"]
    cols = mesh.shape["col"]
    bits = [1 << i for i in range(1, count.bit_length() - 1)]
    crossed, rest = bits[:2], bits[2:]
    stages = [bits[i : i + 2] for i in range(0, len(bits), 2)]
    major = [b for b in rest if b >= cols]
    minor = [b for b in rest if b < cols]
    groups = [part[i : i + 2] for part in (major, minor) for i in range(0, len(part), 2)]
    return jax.shard_map(
        functools.partial(body, groups, crossed, stages, 1, count, cols),
        mesh=mesh,
        in_specs=placed,
        out_specs=(P(None, ("row", "col")), P(None, ("row", "col"))),
        check_vma=False,
    )
```

```python
import functools

import jax
import jax.numpy as jnp
from jax import lax
from jax.experimental import pallas as pl
from jax.experimental.pallas import tpu as pltpu
from jax.sharding import PartitionSpec as P

ITERS = 4
AXES = ("row", "col")
HIGH = lax.Precision.HIGHEST


def nn(left, right):
    return lax.dot_general(
        left, right, (((1,), (0,)), ((), ())), precision=HIGH, preferred_element_type=jnp.float32
    )


def nt(left, right):
    return lax.dot_general(
        left, right, (((1,), (1,)), ((), ())), precision=HIGH, preferred_element_type=jnp.float32
    )


def xor_permute(val, mask, count):
    return lax.ppermute(val, AXES, [(i, i ^ mask) for i in range(count)])


def spread(val, masks, count):
    partners = [0]
    for mask in masks:
        partners = partners + [p ^ mask for p in partners]
    return [val] + [xor_permute(val, p, count) for p in partners[1:]]


def crossed_permute(val, even, odd, core, count):
    return lax.ppermute(val, AXES, [(i, i ^ (odd if i & core else even)) for i in range(count)])


def gather_of(val, groups, crossed, core, count):
    for masks in groups[:-1]:
        val = jnp.concatenate(spread(val, masks, count), axis=0)
    parts = spread(val, groups[-1], count)
    half = len(parts) // 2
    halves = [jnp.concatenate(parts[:half], axis=0), jnp.concatenate(parts[half:], axis=0)]
    one, two = crossed
    near = [crossed_permute(part, one, two, core, count) for part in halves]
    far = [crossed_permute(part, two, one, core, count) for part in halves]
    both = [crossed_permute(part, two, one, core, count) for part in near]
    pieces = halves + near + far + both
    return pieces


def slot_of(me, other, groups, crossed, core):
    diff = me ^ other
    slot = jnp.zeros_like(diff)
    place = 1
    for masks in groups:
        for mask in masks:
            slot = slot + jnp.where((diff & mask) != 0, place, 0)
            place *= 2
    one, two = crossed
    at_one = (other & core) != 0
    first = jnp.where(at_one, diff & two, diff & one) != 0
    second = jnp.where(at_one, diff & one, diff & two) != 0
    slot = slot + jnp.where(first, place, 0) + jnp.where(second, 2 * place, 0)
    return slot + jnp.where((diff & core) != 0, 4 * place, 0)


def matrix_kernel(rows, nbr, blk, count, last, slots, tiles, vec, res, diag, *refs):
    pieces, (image, keep, give, whole) = refs[:count], refs[count:]
    coef = 1.0 / (nbr * blk)
    at = 0
    for piece in pieces:
        whole[at : at + piece.shape[0]] = piece[...]
        at += piece.shape[0]
    n = vec.shape[0]
    for row in range(rows):
        acc = jnp.zeros((n, blk), jnp.float32)
        for k in range(nbr):
            spot = row * nbr + k
            acc = acc + lax.dot_general(
                whole[slots[spot]],
                tiles[row, k],
                (((1,), (1,)), ((), ())),
                preferred_element_type=jnp.float32,
            )
        cols = pl.ds(row * blk, blk)
        image[:, cols] = diag[:, cols] * vec[:, cols] + coef * acc
    img = image[...]
    old = res[...]
    curv = nt(vec[...], img)
    core = slots[rows * nbr]
    if last:
        both = jnp.concatenate([nt(old, old), curv], axis=1)
        first, second = both[0 : n // 2], both[n // 2 : n]
    else:
        both = nt(jnp.concatenate([old, img], axis=0), jnp.concatenate([old, img], axis=0))
        first = jnp.concatenate([both[0:n, 0:n], curv], axis=1)
        second = jnp.concatenate([both[0:n, n : 2 * n], both[n : 2 * n, n : 2 * n]], axis=1)
    keep[...] = jnp.where(core == 0, first, second)
    give[...] = jnp.where(core == 0, second, first)


def round_kernel(source, target, same, sems):
    blk = target.shape[2]
    rows = target.shape[0]
    spans = [pl.ds(row * blk, blk) for row in range(rows)]
    copies = [
        pltpu.make_async_copy(source.at[:, span], same.at[:, span], sems.at[row])
        for row, span in enumerate(spans)
    ]
    for copy in copies:
        copy.start()
    for row in range(rows):
        copies[row].wait()
        target[row] = same[:, spans[row]].astype(jnp.bfloat16)


def round_blocks(source, rows):
    n, width = source.shape
    vmem = pl.BlockSpec(memory_space=pltpu.VMEM)
    return pl.pallas_call(
        round_kernel,
        out_shape=(
            jax.ShapeDtypeStruct((rows, n, width // rows), jnp.bfloat16),
            jax.ShapeDtypeStruct(source.shape, source.dtype),
        ),
        in_specs=[pl.BlockSpec(memory_space=pl.ANY)],
        scratch_shapes=[pltpu.SemaphoreType.DMA((rows,))],
        out_specs=(vmem, vmem),
        compiler_params=pltpu.CompilerParams(vmem_limit_bytes=4 * 1024 * 1024),
        name="round",
    )(pltpu.with_memory_space_constraint(source, pltpu.HBM))


def load_kernel(parts, source, diag, after, target, diag_target, token, sems):
    del after
    rows, nbr = source.shape[:2]
    each = rows * nbr // parts
    copies = [pltpu.make_async_copy(diag, diag_target, sems.at[parts])]
    for part in range(parts):
        row, at = divmod(part * each, nbr)
        span = pl.ds(at, each)
        copies.append(
            pltpu.make_async_copy(source.at[row, span], target.at[row, span], sems.at[part])
        )
    for copy in copies:
        copy.start()
    token[...] = jnp.zeros_like(token)
    for copy in copies:
        copy.wait()


def load(source, diag, after):
    anywhere = pl.BlockSpec(memory_space=pl.ANY)
    vmem = pl.BlockSpec(memory_space=pltpu.VMEM)
    parts = 16
    return pl.pallas_call(
        functools.partial(load_kernel, parts),
        out_shape=(
            jax.ShapeDtypeStruct(source.shape, source.dtype),
            jax.ShapeDtypeStruct(diag.shape, diag.dtype),
            jax.ShapeDtypeStruct((8, 128), jnp.float32),
        ),
        in_specs=[anywhere] * 3,
        out_specs=(vmem, vmem, vmem),
        scratch_shapes=[pltpu.SemaphoreType.DMA((parts + 1,))],
        compiler_params=pltpu.CompilerParams(vmem_limit_bytes=6 * 1024 * 1024),
        name="load",
    )(
        pltpu.with_memory_space_constraint(source, pltpu.HBM),
        pltpu.with_memory_space_constraint(diag, pltpu.HBM),
        after,
    )


def apply_matrix(last, slots, pieces, tiles, vec, res, diag):
    rows, nbr, blk, _ = tiles.shape
    n = vec.shape[0]
    vmem = pl.BlockSpec(memory_space=pltpu.VMEM)
    blocks = sum(piece.shape[0] for piece in pieces)
    grant = 2 * blocks * n * blk * 2 + tiles.size * 2 + 2 * 1024 * 1024
    half = jax.ShapeDtypeStruct((n // 2 if last else n, 2 * n), jnp.float32)
    outs = [jax.ShapeDtypeStruct(vec.shape, jnp.float32), half, half]
    scratch = [pltpu.VMEM((blocks, n, blk), tiles.dtype)]
    return pl.pallas_call(
        functools.partial(matrix_kernel, rows, nbr, blk, len(pieces), last),
        out_shape=tuple(outs),
        in_specs=[pl.BlockSpec(memory_space=pltpu.SMEM), vmem, vmem, vmem, vmem]
        + [vmem] * len(pieces),
        out_specs=tuple([vmem] * len(outs)),
        scratch_shapes=scratch,
        compiler_params=pltpu.CompilerParams(vmem_limit_bytes=grant),
        name="matrix",
    )(slots, tiles, vec, res, diag, *pieces)


def invert_pair(mats, n):
    size = 8
    width = 2 * n
    lanes = lax.broadcasted_iota(jnp.int32, (size, width), 1)
    rows = lax.broadcasted_iota(jnp.int32, (size, width), 0)
    left = lanes < n
    place = jnp.where(left, lanes, lanes - n)
    line_place = place[0:1, :]
    blocks = [mats[i : i + size, :] for i in range(0, n, size)]
    for at in range(n // size):
        base = at * size
        spread_cols = [
            [
                jnp.where(
                    left,
                    jnp.broadcast_to(block[:, base + i : base + i + 1], (size, width)),
                    jnp.broadcast_to(block[:, n + base + i : n + base + i + 1], (size, width)),
                )
                for i in range(size)
            ]
            for block in blocks
        ]
        own = spread_cols[at]
        inside = (line_place >= base) & (line_place < base + size)
        lines = [
            jnp.where(line_place == base + i, 1.0, jnp.where(inside, 0.0, blocks[at][i : i + 1, :]))
            for i in range(size)
        ]
        upper = [[own[k][i : i + 1, :] if k >= i else None for k in range(size)] for i in range(size)]
        for i in range(size):
            inv = 1.0 / upper[i][i]
            for m in range(i + 1, size):
                factor = upper[i][m] * inv
                for k in range(m, size):
                    upper[m][k] = upper[m][k] - factor * upper[i][k]
                lines[m] = lines[m] - factor * lines[i]
            upper[i][i] = inv
        for i in reversed(range(size)):
            for k in range(i + 1, size):
                lines[i] = lines[i] - upper[i][k] * lines[k]
            lines[i] = lines[i] * upper[i][i]
        within = (place >= base) & (place < base + size)
        solved = jnp.broadcast_to(lines[0], (size, width))
        for i in range(1, size):
            solved = jnp.where(rows == i, jnp.broadcast_to(lines[i], (size, width)), solved)
        for q, block in enumerate(blocks):
            if q == at:
                continue
            kept = jnp.where(within, 0.0, block)
            for i in range(size):
                kept = kept - spread_cols[q][i] * lines[i]
            blocks[q] = kept
        blocks[at] = solved
    return jnp.concatenate(blocks, axis=0)


def solve_kernel(last, core, mine, other, vec, res, sol, image, *outs):
    n = vec.shape[0]
    at_zero = core[0] == 0
    first = jnp.where(at_zero, mine[...], other[...])
    if last:
        first = jnp.concatenate([first, jnp.where(at_zero, other[...], mine[...])], axis=0)
    gram, curv = first[:, 0:n], first[:, n : 2 * n]
    inverses = invert_pair(jnp.concatenate([curv, gram], axis=1), n)
    alpha_t = nn(gram, inverses[:, 0:n])
    old = vec[...]
    new = res[...] - nn(alpha_t, image[...])
    outs[0][...] = sol[...] + nn(alpha_t, old) if last else alpha_t
    outs[1][...] = new
    if not last:
        second = jnp.where(at_zero, other[...], mine[...])
        cross, square = second[:, 0:n], second[:, n : 2 * n]
        mixed = nt(cross, alpha_t)
        gram_new = gram - mixed + nn(alpha_t, nt(square, alpha_t) - cross.T)
        beta_t = nn(gram_new, inverses[:, n : 2 * n])
        step = new + nn(beta_t, old)
        outs[2][...] = step
        blk = outs[3].shape[2]
        for row in range(outs[3].shape[0]):
            outs[3][row] = step[:, row * blk : (row + 1) * blk].astype(jnp.bfloat16)


def solve_step(last, rows, core, mine, other, vec, res, sol, image):
    shape = jax.ShapeDtypeStruct(vec.shape, jnp.float32)
    n, width = vec.shape
    space = pl.BlockSpec(memory_space=pltpu.VMEM)
    outs = [shape, shape]
    if not last:
        outs[0] = jax.ShapeDtypeStruct((n, n), jnp.float32)
        outs += [shape, jax.ShapeDtypeStruct((rows, n, width // rows), jnp.bfloat16)]
    return pl.pallas_call(
        functools.partial(solve_kernel, last),
        out_shape=tuple(outs),
        in_specs=[pl.BlockSpec(memory_space=pltpu.SMEM)] + [space] * 6,
        out_specs=tuple([space] * len(outs)),
        compiler_params=pltpu.CompilerParams(vmem_limit_bytes=8 * 1024 * 1024),
        name="small_last" if last else "small",
    )(core, mine, other, vec, res, sol, image)


def grow_kernel(sol, alpha_t, vec, out):
    out[...] = sol[...] + nn(alpha_t[...], vec[...])


def grow(sol, alpha_t, vec):
    space = pl.BlockSpec(memory_space=pltpu.VMEM)
    return pl.pallas_call(
        grow_kernel,
        out_shape=jax.ShapeDtypeStruct(vec.shape, jnp.float32),
        in_specs=[space] * 3,
        out_specs=space,
        compiler_params=pltpu.CompilerParams(vmem_limit_bytes=4 * 1024 * 1024),
        name="grow",
    )(sol, alpha_t, vec)


def body(groups, crossed, stages, core_bit, count, cols, right_side, diag_vals, tiles, col_ids):
    rows, nbr, blk, _ = tiles.shape
    me = lax.axis_index("row") * cols + lax.axis_index("col")
    core = ((me & core_bit) != 0).astype(jnp.int32)[None]
    ids = col_ids.reshape(-1)
    slots = slot_of(me, ids // rows, groups, crossed, core_bit) * rows + ids % rows
    slots = jnp.concatenate([slots, core])
    diag = diag_vals[None, :]
    sol = jnp.zeros_like(right_side)
    rounded, res = round_blocks(right_side, rows)
    vec = res
    for step in range(ITERS):
        last = step + 1 == ITERS
        pieces = gather_of(rounded, groups, crossed, core_bit, count)
        if step == 0:
            tiles, diag, token = load(tiles, diag, pieces[3])
            pieces[5], _ = lax.optimization_barrier((pieces[5], token))
        pieces += [xor_permute(piece, core_bit, count) for piece in pieces]
        image, keep, give = apply_matrix(last, slots, pieces, tiles, vec, res, diag)
        mine = keep + xor_permute(give, core_bit, count)
        for masks in stages:
            terms = spread(mine, masks, count)
            while len(terms) > 1:
                terms = [left + right for left, right in zip(terms[0::2], terms[1::2])]
            mine = terms[0]
        other = xor_permute(mine, core_bit, count)
        outs = solve_step(last, rows, core, mine, other, vec, res, sol, image)
        if last:
            sol, res = outs
        else:
            alpha_t, res, step_vec, rounded = outs
            sol = grow(sol, alpha_t, vec)
            vec = step_vec
    return (sol, res)


def solution(mesh):
    placed = (
        P(None, ("row", "col")),
        P(("row", "col")),
        P(("row", "col"), None, None, None),
        P(("row", "col"), None),
    )
    count = mesh.shape["row"] * mesh.shape["col"]
    cols = mesh.shape["col"]
    bits = [1 << i for i in range(1, count.bit_length() - 1)]
    crossed, rest = bits[:2], bits[2:]
    stages = [bits[i : i + 2] for i in range(0, len(bits), 2)]
    major = [b for b in rest if b >= cols]
    minor = [b for b in rest if b < cols]
    groups = [part[i : i + 2] for part in (major, minor) for i in range(0, len(part), 2)]
    return jax.shard_map(
        functools.partial(body, groups, crossed, stages, 1, count, cols),
        mesh=mesh,
        in_specs=placed,
        out_specs=(P(None, ("row", "col")), P(None, ("row", "col"))),
        check_vma=False,
    )
```
